32 devices in a mesh: wafer: 2 (over x), die: 16 (over z, y, core).
Axes of the slice: x: 2, y: 2, z: 4, core: 2. Of those that a mesh axis runs over, the one named last changes fastest.
Arguments:
- die_tiles: float32 [512, 64, 1024], P(('wafer', 'die')), parts along dimension 0, may hold values from -14 to 14
- slot_pos: int32 [512], P(('wafer', 'die')), parts along dimension 0, may hold values from 0 to 31, as said below
- slot_die: int32 [512], P(('wafer', 'die')), parts along dimension 0, may hold values from 0 to 7
- present: int32 [16, 32], P('wafer'), parts along dimension 0, may hold values from 0 to 1, as said below
- strength: float32 [32, 64, 1024], P('die'), may hold values from 0.3 to 3
- kernel: float32 [5, 5], replicated, may hold values from 0.1 to 1
Outputs:
- residual: float32 [512, 64, 1024], P(('wafer', 'die')), parts along dimension 0
The draws below stay inside these ranges and needn't reach their ends.
There are 2 independent parts, one for each index of `wafer`. The reference program is written for one: setup_inputs(seed, part) draws one part's arguments, and reference() takes and returns one part's arrays. A program takes and returns all parts, laid end to end along the dimension named above; an argument that names none is the same for every part. Nothing has to cross between parts.
Inputs may be any that keep to these rules, and one draw needn't show every extreme that they name: `slot_pos`: each pair of position and die stands in exactly one slot. Among the slots of one device, at most 2 hold positions with equal position // 2, and this most is reached on every device; every value of position // 2 is held by 16 slots in all. At every position at least 6 dies are present.
All inputs are finite; a program needn't handle non-finite values.
Results may differ from the reference program's by a relative error of at most 0.0001.
Values sent between devices are 32-bit elements; how exact they have to be, the bound alone decides.
A program may use at most 128 MiB of HBM per device.

```python
import math
import jax
import jax.numpy as jnp

COLS = 1024
ROWS = 64
POS_DEV = 2
ITERS = 3
SLOTS = 16
TILES = 256
POSITIONS = 32
DIES = 8


def layout(key):
    count = SLOTS
    base = jax.random.fold_in(key, 11)
    first = jax.random.fold_in(base, 1)
    second = jax.random.fold_in(base, 2)
    third = jax.random.fold_in(base, 3)
    sigma = jax.random.permutation(first, count)
    index = jnp.arange(count, dtype=jnp.int32)
    offset = (index[None, :] - sigma[:, None]) % count
    quarter = count // 4
    counts = 1 + (offset < quarter).astype(jnp.int32) - ((offset >= quarter) & (offset < 2 * quarter)).astype(jnp.int32)
    cumul = jnp.cumsum(counts, axis=0)
    dealt = jax.vmap(lambda sub: jax.random.permutation(sub, count))(jax.random.split(second, count))
    source = jnp.sum((cumul.T[:, :, None] <= index[None, None, :]).astype(jnp.int32), axis=1)
    start = (cumul - counts).T
    within = index[None, :] - jnp.take_along_axis(start, source, axis=1)
    before = (jnp.cumsum(counts, axis=1) - counts).T
    source_rank = jnp.take_along_axis(before, source, axis=1) + within
    shuffle = jax.vmap(lambda sub: jax.random.permutation(sub, count))(jax.random.split(third, count))
    local_slot = shuffle[source.ravel(), source_rank.ravel()]
    global_slot = source.ravel() * count + local_slot
    owner = jnp.repeat(index, count)
    tile_id = dealt.ravel()
    position = owner * POS_DEV + tile_id // DIES
    die_id = tile_id % DIES
    slot_position = jnp.zeros((TILES,), jnp.int32).at[global_slot].set(position.astype(jnp.int32))
    slot_dies = jnp.zeros((TILES,), jnp.int32).at[global_slot].set(die_id.astype(jnp.int32))
    return (slot_position, slot_dies)


def draw_slot_pos(key, part):
    return layout(key)[0]


def draw_slot_die(key, part):
    return layout(key)[1]


def draw_present(key, part):
    first = jax.random.fold_in(key, 21)
    second = jax.random.fold_in(key, 22)
    edge = jax.random.permutation(first, DIES) < DIES // 4
    coin = jax.random.randint(second, (DIES, POSITIONS), 0, 2)
    return jnp.where(edge[:, None], coin, 1).astype(jnp.int32)


def draw_die_tiles(key, part):
    slot_position = layout(key)[0]
    pattern = jnp.clip(1.5 * jax.random.normal(jax.random.fold_in(key, 31), (POSITIONS, ROWS, COLS), jnp.float32), -5.0, 5.0)
    noise = jnp.clip(0.5 * jax.random.normal(jax.random.fold_in(key, 32), (TILES, ROWS, COLS), jnp.float32), -2.5, 2.5)
    chance = jax.random.uniform(jax.random.fold_in(key, 33), (TILES, ROWS, COLS), jnp.float32)
    height = jax.random.uniform(jax.random.fold_in(key, 34), (TILES, ROWS, COLS), jnp.float32, 1.5, 4.0)
    flip = jnp.where(jax.random.uniform(jax.random.fold_in(key, 35), (TILES, ROWS, COLS), jnp.float32) < 0.15, -1.0, 1.0)
    defect = jnp.where(chance < 0.3, flip * height, 0.0)
    return (pattern[slot_position] + noise + defect).astype(jnp.float32)


def level_of(rng, dims, cuts, least, high):
    factor_of, own = 1.0, jax.random.fold_in(rng, 6)
    for dim, blocks in cuts:
        heights = jnp.exp(jax.random.uniform(jax.random.fold_in(own, dim), (blocks,), jnp.float32, least / len(cuts), high / len(cuts)))
        factor_of = factor_of * jnp.repeat(heights, dims[dim] // blocks).reshape([-1 if axis == dim else 1 for axis in range(len(dims))])
    return factor_of


def setup_inputs(seed: int = 0, part: int = 0) -> dict:
    keys = jax.random.split(jax.random.key(seed), 7)
    part_keys = jax.random.split(jax.random.fold_in(keys[6], part), 7)
    die_tiles = draw_die_tiles(jax.random.fold_in(jax.random.fold_in(keys[6], part), 71), part)
    slot_pos = draw_slot_pos(jax.random.fold_in(jax.random.fold_in(keys[6], part), 71), part)
    slot_die = draw_slot_die(jax.random.fold_in(jax.random.fold_in(keys[6], part), 71), part)
    present = draw_present(jax.random.fold_in(jax.random.fold_in(keys[6], part), 71), part)
    strength = jnp.clip(jnp.exp(math.log(3.0) - 2.3025851 * jax.random.uniform(keys[4], (POSITIONS, ROWS, COLS), jnp.float32) ** level_of(keys[4], (POSITIONS, ROWS, COLS), ((0, 16),), -0.2, 0.2)), 0.3, 3.0)
    kernel = jnp.clip(jax.random.uniform(keys[5], (5, 5), jnp.float32, 0.1, 1.0), 0.1, 1.0)
    return dict(die_tiles=die_tiles, slot_pos=slot_pos, slot_die=slot_die, present=present, strength=strength, kernel=kernel)


def smooth(field, strength, kernel):
    rows = field.shape[1]
    cols = field.shape[2]
    padded = jnp.pad(field, ((0, 0), (2, 2), (2, 2)))
    total = jnp.zeros_like(field)
    for shift_row in range(5):
        for shift_col in range(5):
            total = total + kernel[shift_row, shift_col] * padded[:, shift_row:shift_row + rows, shift_col:shift_col + cols]
    return (field + strength * total) / (1.0 + strength * jnp.sum(kernel))


def reference(die_tiles, slot_pos, slot_die, present, strength, kernel):
    rows = die_tiles.shape[1]
    cols = die_tiles.shape[2]
    pair = (slot_pos * DIES + slot_die).astype(jnp.int32)
    where_slot = jnp.zeros((TILES,), jnp.int32).at[pair].set(jnp.arange(TILES, dtype=jnp.int32))
    stack = die_tiles[where_slot].reshape(POSITIONS, DIES, rows, cols)
    live = present.T.astype(jnp.float32)
    weight0 = live[:, :, None, None]
    mean = jnp.sum(weight0 * stack, axis=1) / jnp.sum(live, axis=1)[:, None, None]
    refer = mean
    for step in range(ITERS):
        gap = jnp.abs(stack - refer[:, None])
        weight = weight0 * 1.5 / jnp.maximum(gap, 1.5)
        mean = jnp.sum(weight * stack, axis=1) / jnp.sum(weight, axis=1)
        refer = smooth(mean, strength, kernel)
    keep = present[slot_die, slot_pos].astype(jnp.float32)
    return keep[:, None, None] * (die_tiles - refer[slot_pos])
```

```python
import functools

import jax
import jax.numpy as jnp
from jax import lax
from jax.experimental import pallas as pl
from jax.experimental.pallas import tpu as pltpu
from jax.sharding import PartitionSpec as P

ITERS = 3
RS = 8
LANES = 128


def strip_of(q, strips):
    odd = q % 2
    half = q // 2
    return half * (1 - odd) + (strips - 1 - half) * odd


def chip_of(s, strips):
    high = s // (strips // 2)
    return 2 * s * (1 - high) + (2 * (strips - 1 - s) + 1) * high


def greet(n):
    me = lax.axis_index("die")
    barrier = pltpu.get_barrier_semaphore()
    for k in range(1, n):
        pl.semaphore_signal(barrier, inc=1, device_id={"die": (me + k) % n}, device_id_type=pl.DeviceIdType.MESH)
    pl.semaphore_wait(barrier, n - 1)


def remote(src, dst, send, recv, device):
    return pltpu.make_async_remote_copy(
        src_ref=src, dst_ref=dst, send_sem=send, recv_sem=recv,
        device_id={"die": device}, device_id_type=pl.DeviceIdType.MESH,
    )


def scatter_kernel(n, strips, blocks, cs, tiles, strength, arrived, power, send, recv, psend, precv, own):
    me = lax.axis_index("die")

    def region(device):
        s = strip_of(device // blocks, strips)
        c = device % blocks
        return pl.ds(pl.multiple_of(s * RS, RS), RS), pl.ds(pl.multiple_of(c * cs, LANES), cs)

    greet(n)
    copies = []
    for k in range(1, n):
        peer = (me + k) % n
        rows, cols = region(peer)
        copies.append(remote(tiles.at[:, rows, cols], arrived.at[me], send.at[k], recv.at[k], peer))
        copies[-1].start()
    for k in range(1, n):
        peer = (me + k) % n
        rows, cols = region(peer)
        copies.append(remote(strength.at[:, rows, cols], power.at[me], psend.at[k], precv.at[k], peer))
        copies[-1].start()
    rows, cols = region(me)
    copies.append(pltpu.make_async_copy(tiles.at[:, rows, cols], arrived.at[me], own.at[0]))
    copies[-1].start()
    copies.append(pltpu.make_async_copy(strength.at[:, rows, cols], power.at[me], own.at[1]))
    copies[-1].start()
    for copy in copies:
        copy.wait()


def refer_kernel(
    n, strips, blocks, cs, dies, positions,
    where, live, kern, arrived, power, out,
    stack, strength, mean, top, bottom, rows_up, rows_down, side_left, side_right, corners, ext, refer,
    load, hsend, hrecv, rsend, rrecv, ssend, srecv, own,
):
    me = lax.axis_index("die")
    s = strip_of(me // blocks, strips)
    c = me % blocks
    groups = positions // 4

    def device(ds, dc):
        return chip_of((s + ds + strips) % strips, strips) * blocks + (c + dc + blocks) % blocks

    loads = [
        pltpu.make_async_copy(arrived, stack, load.at[0]),
        pltpu.make_async_copy(power, strength, load.at[1]),
    ]
    for copy in loads:
        copy.start()
    greet(n)
    for copy in loads:
        copy.wait()

    first = pl.ds(0, LANES)
    last = pl.ds(cs - LANES, LANES)
    taps = [[kern[5 * a + b] for b in range(5)] for a in range(5)]
    total = taps[0][0]
    for a in range(5):
        for b in range(5):
            if a or b:
                total = total + taps[a][b]

    def exchange(k):
        copies = [
            remote(bottom.at[k], rows_up.at[k], hsend.at[k, 0], hrecv.at[k, 0], device(1, 0)),
            remote(top.at[k], rows_down.at[k], hsend.at[k, 1], hrecv.at[k, 1], device(-1, 0)),
            remote(mean.at[k, :, :, last], side_left.at[k], hsend.at[k, 2], hrecv.at[k, 2], device(0, 1)),
            remote(mean.at[k, :, :, first], side_right.at[k], hsend.at[k, 3], hrecv.at[k, 3], device(0, -1)),
            remote(bottom.at[k, :, :, last], corners.at[k, 0], hsend.at[k, 4], hrecv.at[k, 4], device(1, 1)),
            remote(bottom.at[k, :, :, first], corners.at[k, 1], hsend.at[k, 5], hrecv.at[k, 5], device(1, -1)),
            remote(top.at[k, :, :, last], corners.at[k, 2], hsend.at[k, 6], hrecv.at[k, 6], device(-1, 1)),
            remote(top.at[k, :, :, first], corners.at[k, 3], hsend.at[k, 7], hrecv.at[k, 7], device(-1, -1)),
        ]
        for copy in copies:
            copy.start()
        for copy in copies:
            copy.wait()

    def guard(flag, x):
        return jnp.where(flag, x, jnp.zeros_like(x))

    has_up, has_down, has_left, has_right = s > 0, s < strips - 1, c > 0, c < blocks - 1
    body = pl.ds(LANES, cs)
    right = pl.ds(LANES + cs, LANES)

    def smooth(k, g, j):
        p = 4 * g + j
        pair = pl.ds(2 * j, 2)
        field = mean[k, p]
        ext[j, 6:8, first] = guard(has_up & has_left, corners[k, 0, g, pair, :])
        ext[j, 6:8, body] = guard(has_up, rows_up[k, g, pair, :])
        ext[j, 6:8, right] = guard(has_up & has_right, corners[k, 1, g, pair, :])
        ext[j, 8:16, first] = guard(has_left, side_left[k, p])
        ext[j, 8:16, body] = field
        ext[j, 8:16, right] = guard(has_right, side_right[k, p])
        ext[j, 16:18, first] = guard(has_down & has_left, corners[k, 2, g, pair, :])
        ext[j, 16:18, body] = guard(has_down, rows_down[k, g, pair, :])
        ext[j, 16:18, right] = guard(has_down & has_right, corners[k, 3, g, pair, :])
        shifted = [ext[j, 6 + a : 14 + a, :] for a in range(5)]
        width = cs + 2 * LANES
        acc = None
        for b in range(5):
            part = shifted[0] * taps[0][b]
            for a in range(1, 5):
                part = part + shifted[a] * taps[a][b]
            if b != 2:
                part = pltpu.roll(part, (2 - b) % width, 1)
            part = part[:, LANES : LANES + cs]
            acc = part if acc is None else acc + part
        power_p = strength[p]
        return (field + power_p * acc) / (1.0 + power_p * total)

    def huber(k, g, j, ref):
        p = 4 * g + j
        num = None
        for d in range(dies):
            value = stack[where[p * dies + d]]
            weight = live[p * dies + d] / jnp.maximum(jnp.abs(value - ref), 1.5)
            num, den = (weight * value, weight) if num is None else (num + weight * value, den + weight)
        field = num / den
        mean[k, p] = field
        top[k, g, 2 * j : 2 * j + 2, :] = field[0:2]
        bottom[k, g, 2 * j : 2 * j + 2, :] = field[RS - 2 : RS]

    @pl.loop(0, groups)
    def _(g):
        for j in range(4):
            p = 4 * g + j
            count = live[p * dies]
            num = count * stack[where[p * dies]]
            for d in range(1, dies):
                share = live[p * dies + d]
                count = count + share
                num = num + share * stack[where[p * dies + d]]
            huber(0, g, j, num / jnp.full(num.shape, count))

    for k in range(1, ITERS):
        exchange(k - 1)

        @pl.loop(0, groups)
        def _(g):
            for j in range(4):
                huber(k, g, j, smooth(k - 1, g, j))

    exchange(ITERS - 1)

    @pl.loop(0, groups)
    def _(g):
        for j in range(4):
            refer[4 * g + j] = smooth(ITERS - 1, g, j)

    turn = 1 - 2 * (c % 2)
    ahead = device(turn, 0)
    mine = pltpu.make_async_copy(refer, out.at[s, c], own)
    mine.start()
    pending = []
    for t in range(strips):
        strip = (s - turn * t + strips) % strips
        block = refer if t == 0 else out.at[strip, c]
        if t:
            ring.wait_recv()
        if t < strips - 1:
            ring = remote(block, out.at[strip, c], rsend.at[t], rrecv.at[t], ahead)
            ring.start()
            pending.append(ring)
        for b in range(1, blocks):
            side = remote(block, out.at[strip, c], ssend.at[t, b], srecv.at[t, b], device(0, b))
            side.start()
            pending.append(side)
    for copy in pending:
        copy.wait_send()
    for t in range(strips):
        for b in range(1, blocks):
            source = (c - b + blocks) % blocks
            strip = (s - (1 - 2 * (source % 2)) * t + strips) % strips
            remote(out.at[strip, source], out.at[strip, source], ssend.at[t, b], srecv.at[t, b], device(0, b)).wait_recv()
    mine.wait()


def residual_kernel(strips, blocks, cs, pos, die, present, tile, refer, out):
    i = pl.program_id(0)
    keep = present[die[i], pos[i]].astype(jnp.float32)
    for s in range(strips):
        for c in range(blocks):
            rows, cols = pl.ds(s * RS, RS), pl.ds(c * cs, cs)
            out[0, rows, cols] = keep * (tile[0, rows, cols] - refer[s, c, 0])


def shards(n, die_tiles, slot_pos, slot_die, present, strength, kernel):
    slots, rows, cols = die_tiles.shape
    dies, positions = present.shape
    local = strength.shape[0]
    strips = rows // RS
    blocks = n // strips
    cs = cols // blocks
    hbm = pl.BlockSpec(memory_space=pl.ANY)
    smem = pl.BlockSpec(memory_space=pltpu.SMEM)
    dma = pltpu.SemaphoreType.DMA
    f32 = jnp.float32

    pair = slot_pos * dies + slot_die
    pairs = lax.all_gather(pair, "die", axis=0, tiled=True)
    count = positions * dies
    order = jnp.arange(n * slots, dtype=jnp.int32)
    where = jnp.sum(jnp.where(pairs[None, :] == jnp.arange(count, dtype=jnp.int32)[:, None], order[None, :], 0), axis=1)

    arrived, power = pl.pallas_call(
        functools.partial(scatter_kernel, n, strips, blocks, cs),
        name="scatter",
        out_shape=(
            jax.ShapeDtypeStruct((n, slots, RS, cs), f32),
            jax.ShapeDtypeStruct((n, local, RS, cs), f32),
        ),
        in_specs=[hbm, hbm],
        out_specs=(hbm, hbm),
        scratch_shapes=[dma((n,)), dma((n,)), dma((n,)), dma((n,)), dma((2,))],
        compiler_params=pltpu.CompilerParams(collective_id=0, has_side_effects=True),
    )(die_tiles, strength)

    groups = positions // 4
    vmem = pltpu.VMEM
    refer = pl.pallas_call(
        functools.partial(refer_kernel, n, strips, blocks, cs, dies, positions),
        name="refer",
        out_shape=jax.ShapeDtypeStruct((strips, blocks, positions, RS, cs), f32),
        in_specs=[smem, smem, smem, hbm, hbm],
        out_specs=hbm,
        scratch_shapes=[
            vmem((n * slots, RS, cs), f32),
            vmem((positions, RS, cs), f32),
            vmem((ITERS, positions, RS, cs), f32),
            vmem((ITERS, groups, 8, cs), f32),
            vmem((ITERS, groups, 8, cs), f32),
            vmem((ITERS, groups, 8, cs), f32),
            vmem((ITERS, groups, 8, cs), f32),
            vmem((ITERS, positions, RS, LANES), f32),
            vmem((ITERS, positions, RS, LANES), f32),
            vmem((ITERS, 4, groups, 8, LANES), f32),
            vmem((4, 24, cs + 2 * LANES), f32),
            vmem((positions, RS, cs), f32),
            dma((2,)),
            dma((ITERS, 8)),
            dma((ITERS, 8)),
            dma((strips,)),
            dma((strips,)),
            dma((strips, blocks)),
            dma((strips, blocks)),
            dma,
        ],
        compiler_params=pltpu.CompilerParams(
            collective_id=1, has_side_effects=True, vmem_limit_bytes=40 * 1024 * 1024
        ),
    )(
        where,
        present.T.astype(f32).reshape(count),
        kernel.reshape(25),
        arrived.reshape(n * slots, RS, cs),
        power.reshape(positions, RS, cs),
    )

    return pl.pallas_call(
        functools.partial(residual_kernel, strips, blocks, cs),
        name="residual",
        out_shape=jax.ShapeDtypeStruct((slots, rows, cols), f32),
        grid_spec=pltpu.PrefetchScalarGridSpec(
            num_scalar_prefetch=3,
            grid=(slots,),
            in_specs=[
                pl.BlockSpec((1, rows, cols), lambda i, *_: (i, 0, 0)),
                pl.BlockSpec((strips, blocks, 1, RS, cs), lambda i, pos, *_: (0, 0, pos[i], 0, 0)),
            ],
            out_specs=pl.BlockSpec((1, rows, cols), lambda i, *_: (i, 0, 0)),
        ),
    )(slot_pos, slot_die, present, die_tiles, refer)


def solution(mesh):
    placed = (
        P(("wafer", "die"), None, None),
        P(("wafer", "die")),
        P(("wafer", "die")),
        P("wafer", None),
        P("die", None, None),
        P(),
    )
    return jax.shard_map(
        functools.partial(shards, mesh.shape["die"]),
        mesh=mesh,
        in_specs=placed,
        out_specs=P(("wafer", "die"), None, None),
        check_vma=False,
    )
```

```python
import functools

import jax
import jax.numpy as jnp
from jax import lax
from jax.experimental import pallas as pl
from jax.experimental.pallas import tpu as pltpu
from jax.sharding import PartitionSpec as P

ITERS = 3
RS = 8
LANES = 128
PARTS = 4


def strip_of(q, strips):
    odd = q % 2
    half = q // 2
    return half * (1 - odd) + (strips - 1 - half) * odd


def chip_of(s, strips):
    high = s // (strips // 2)
    return 2 * s * (1 - high) + (2 * (strips - 1 - s) + 1) * high


def greet(n):
    me = lax.axis_index("die")
    barrier = pltpu.get_barrier_semaphore()
    for k in range(1, n):
        pl.semaphore_signal(barrier, inc=1, device_id={"die": (me + k) % n}, device_id_type=pl.DeviceIdType.MESH)
    pl.semaphore_wait(barrier, n - 1)


def remote(src, dst, send, recv, device):
    return pltpu.make_async_remote_copy(
        src_ref=src, dst_ref=dst, send_sem=send, recv_sem=recv,
        device_id={"die": device}, device_id_type=pl.DeviceIdType.MESH,
    )


def refer_kernel(
    n, strips, blocks, cs, dies, positions,
    live, kern, pair, tiles, power, out,
    stacks, strength, pairs, table, where, mean,
    top, bottom, rows_up, rows_down, side_left, side_right, corners, ext, refer,
    send, recv, psend, precv, qsend, qrecv, local, hsend, hrecv, rsend, rrecv, ssend, srecv, own,
):
    me = lax.axis_index("die")
    slots = tiles.shape[0]
    held = power.shape[0]
    chunks = cs // LANES
    s = strip_of(me // blocks, strips)
    c = me % blocks
    groups = positions // 4

    def device(ds, dc):
        return chip_of((s + ds + strips) % strips, strips) * blocks + (c + dc + blocks) % blocks

    def rows_of(peer):
        return pl.ds(pl.multiple_of(strip_of(peer // blocks, strips) * RS, RS), RS)

    def cols_of(peer, start, size):
        return pl.ds(pl.multiple_of((peer % blocks) * cs + start, LANES), size)

    tile_rows = pl.ds(me * slots, slots)
    power_rows = pl.ds(me * held, held)
    greet(n)
    pair_copies = [pltpu.make_async_copy(pair, pairs.at[tile_rows], local.at[0])]
    for k in range(1, n):
        pair_copies.append(remote(pair, pairs.at[tile_rows], qsend.at[k], qrecv.at[k], (me + k) % n))
    for copy in pair_copies:
        copy.start()
    tile_copies = []
    for u in range(chunks):
        wave = [
            pltpu.make_async_copy(
                tiles.at[:, rows_of(me), cols_of(me, u * LANES, LANES)], stacks[u].at[tile_rows], local.at[2 + u]
            )
        ]
        for k in range(1, n):
            peer = (me + k) % n
            wave.append(
                remote(
                    tiles.at[:, rows_of(peer), cols_of(peer, u * LANES, LANES)], stacks[u].at[tile_rows],
                    send.at[u, k], recv.at[u, k], peer,
                )
            )
        for copy in wave:
            copy.start()
        tile_copies.append(wave)
    power_copies = [
        pltpu.make_async_copy(power.at[:, rows_of(me), cols_of(me, 0, cs)], strength.at[power_rows], local.at[1])
    ]
    for k in range(1, n):
        peer = (me + k) % n
        power_copies.append(
            remote(
                power.at[:, rows_of(peer), cols_of(peer, 0, cs)], strength.at[power_rows],
                psend.at[k], precv.at[k], peer,
            )
        )
    for copy in power_copies:
        copy.start()

    for copy in pair_copies:
        copy.wait()
    order = lax.broadcasted_iota(jnp.int32, (n * slots, LANES), 0)
    target = lax.broadcasted_iota(jnp.int32, (n * slots, LANES), 1)
    for w in range(table.shape[0]):
        hit = pairs[...] == target + w * LANES
        table[w : w + 1, :] = jnp.max(jnp.where(hit, order, 0), axis=0, keepdims=True)
    fetch = pltpu.make_async_copy(table, where, local.at[2 + chunks])
    fetch.start()
    fetch.wait()

    def value_of(p, d, some):
        q = p * dies + d
        entry = where[q // LANES, q % LANES]
        if len(some) == 1:
            return stacks[some[0]][entry]
        return jnp.concatenate([stacks[u][entry] for u in some], axis=1)

    first = pl.ds(0, LANES)
    last = pl.ds(cs - LANES, LANES)
    taps = [[kern[5 * a + b] for b in range(5)] for a in range(5)]
    total = taps[0][0]
    for a in range(5):
        for b in range(5):
            if a or b:
                total = total + taps[a][b]

    def exchange(k):
        copies = [
            remote(bottom.at[k], rows_up.at[k], hsend.at[k, 0], hrecv.at[k, 0], device(1, 0)),
            remote(top.at[k], rows_down.at[k], hsend.at[k, 1], hrecv.at[k, 1], device(-1, 0)),
            remote(mean.at[k, :, :, last], side_left.at[k], hsend.at[k, 2], hrecv.at[k, 2], device(0, 1)),
            remote(mean.at[k, :, :, first], side_right.at[k], hsend.at[k, 3], hrecv.at[k, 3], device(0, -1)),
            remote(bottom.at[k, :, :, last], corners.at[k, 0], hsend.at[k, 4], hrecv.at[k, 4], device(1, 1)),
            remote(bottom.at[k, :, :, first], corners.at[k, 1], hsend.at[k, 5], hrecv.at[k, 5], device(1, -1)),
            remote(top.at[k, :, :, last], corners.at[k, 2], hsend.at[k, 6], hrecv.at[k, 6], device(-1, 1)),
            remote(top.at[k, :, :, first], corners.at[k, 3], hsend.at[k, 7], hrecv.at[k, 7], device(-1, -1)),
        ]
        for copy in copies:
            copy.start()
        for copy in copies:
            copy.wait()

    def guard(flag, x):
        return jnp.where(flag, x, jnp.zeros_like(x))

    has_up, has_down, has_left, has_right = s > 0, s < strips - 1, c > 0, c < blocks - 1
    body = pl.ds(LANES, cs)
    right = pl.ds(LANES + cs, LANES)

    def smooth(k, g, j):
        p = 4 * g + j
        pair = pl.ds(2 * j, 2)
        field = mean[k, p]
        ext[j, 6:8, first] = guard(has_up & has_left, corners[k, 0, g, pair, :])
        ext[j, 6:8, body] = guard(has_up, rows_up[k, g, pair, :])
        ext[j, 6:8, right] = guard(has_up & has_right, corners[k, 1, g, pair, :])
        ext[j, 8:16, first] = guard(has_left, side_left[k, p])
        ext[j, 8:16, body] = field
        ext[j, 8:16, right] = guard(has_right, side_right[k, p])
        ext[j, 16:18, first] = guard(has_down & has_left, corners[k, 2, g, pair, :])
        ext[j, 16:18, body] = guard(has_down, rows_down[k, g, pair, :])
        ext[j, 16:18, right] = guard(has_down & has_right, corners[k, 3, g, pair, :])
        shifted = [ext[j, 6 + a : 14 + a, :] for a in range(5)]
        width = cs + 2 * LANES
        acc = None
        for b in range(5):
            part = shifted[0] * taps[0][b]
            for a in range(1, 5):
                part = part + shifted[a] * taps[a][b]
            if b != 2:
                part = pltpu.roll(part, (2 - b) % width, 1)
            part = part[:, LANES : LANES + cs]
            acc = part if acc is None else acc + part
        power_p = strength[p]
        return (field + power_p * acc) / (1.0 + power_p * total)

    def huber(k, g, j, ref, some):
        lanes = pl.ds(some[0] * LANES, len(some) * LANES)
        p = 4 * g + j
        num = None
        for d in range(dies):
            value = value_of(p, d, some)
            weight = live[p * dies + d] / jnp.maximum(jnp.abs(value - ref), 1.5)
            num, den = (weight * value, weight) if num is None else (num + weight * value, den + weight)
        field = num / den
        mean[k, p, :, lanes] = field
        top[k, g, 2 * j : 2 * j + 2, lanes] = field[0:2]
        bottom[k, g, 2 * j : 2 * j + 2, lanes] = field[RS - 2 : RS]

    for u in range(chunks):
        some = (u,)
        for copy in tile_copies[u]:
            copy.wait()

        @pl.loop(0, groups)
        def _(g):
            for j in range(4):
                p = 4 * g + j
                count = live[p * dies]
                num = count * value_of(p, 0, some)
                for d in range(1, dies):
                    share = live[p * dies + d]
                    count = count + share
                    num = num + share * value_of(p, d, some)
                huber(0, g, j, num / jnp.full(num.shape, count), some)

    for copy in power_copies:
        copy.wait()

    for k in range(1, ITERS):
        exchange(k - 1)

        @pl.loop(0, groups)
        def _(g):
            for j in range(4):
                huber(k, g, j, smooth(k - 1, g, j), tuple(range(chunks)))

    exchange(ITERS - 1)

    turn = 1 - 2 * (c % 2)
    ahead = device(turn, 0)
    parts = rsend.shape[1]
    span = positions // parts
    pending = []
    rings = {}
    mine = []

    def forward(t, h):
        strip = (s - turn * t + strips) % strips
        part = pl.ds(h * span, span)
        target = out.at[strip, c, part]
        block = target if t else refer.at[part]
        if t:
            rings[t - 1, h].wait_recv()
        copies = [remote(block, target, ssend.at[t, h, b], srecv.at[t, h, b], device(0, b)) for b in range(1, blocks)]
        if t < strips - 1:
            rings[t, h] = remote(block, target, rsend.at[t, h], rrecv.at[t, h], ahead)
            copies.insert(0, rings[t, h])
        for copy in copies:
            copy.start()
        pending.extend(copies)

    for h in range(parts):

        @pl.loop(h * span // 4, (h + 1) * span // 4)
        def _(g):
            for j in range(4):
                refer[4 * g + j] = smooth(ITERS - 1, g, j)

        part = pl.ds(h * span, span)
        mine.append(pltpu.make_async_copy(refer.at[part], out.at[s, c, part], own.at[h]))
        mine[-1].start()
        forward(0, h)
    for t in range(1, strips):
        for h in range(parts):
            forward(t, h)
    for copy in pending:
        copy.wait_send()
    for t in range(strips):
        for h in range(parts):
            for b in range(1, blocks):
                source = (c - b + blocks) % blocks
                strip = (s - (1 - 2 * (source % 2)) * t + strips) % strips
                target = out.at[strip, source, pl.ds(h * span, span)]
                remote(target, target, ssend.at[t, h, b], srecv.at[t, h, b], device(0, b)).wait_recv()
    for copy in mine:
        copy.wait()


def residual_kernel(strips, blocks, cs, pos, die, present, tile, refer, out):
    i = pl.program_id(0)
    keep = present[die[i], pos[i]].astype(jnp.float32)
    for s in range(strips):
        for c in range(blocks):
            rows, cols = pl.ds(s * RS, RS), pl.ds(c * cs, cs)
            out[0, rows, cols] = keep * (tile[0, rows, cols] - refer[s, c, 0])


def shards(n, die_tiles, slot_pos, slot_die, present, strength, kernel):
    slots, rows, cols = die_tiles.shape
    dies, positions = present.shape
    strips = rows // RS
    blocks = n // strips
    cs = cols // blocks
    hbm = pl.BlockSpec(memory_space=pl.ANY)
    smem = pl.BlockSpec(memory_space=pltpu.SMEM)
    dma = pltpu.SemaphoreType.DMA
    f32 = jnp.float32

    count = positions * dies
    chunks = cs // LANES
    pair = jnp.broadcast_to((slot_pos * dies + slot_die)[:, None], (slots, LANES))
    groups = positions // 4
    vmem = pltpu.VMEM
    refer = pl.pallas_call(
        functools.partial(refer_kernel, n, strips, blocks, cs, dies, positions),
        name="refer",
        out_shape=jax.ShapeDtypeStruct((strips, blocks, positions, RS, cs), f32),
        in_specs=[smem, smem, pl.BlockSpec(memory_space=pltpu.VMEM), hbm, hbm],
        out_specs=hbm,
        scratch_shapes=[
            tuple(vmem((n * slots, RS, LANES), f32) for _ in range(chunks)),
            vmem((positions, RS, cs), f32),
            vmem((n * slots, LANES), jnp.int32),
            vmem((count // LANES, LANES), jnp.int32),
            pltpu.SMEM((count // LANES, LANES), jnp.int32),
            vmem((ITERS, positions, RS, cs), f32),
            vmem((ITERS, groups, 8, cs), f32),
            vmem((ITERS, groups, 8, cs), f32),
            vmem((ITERS, groups, 8, cs), f32),
            vmem((ITERS, groups, 8, cs), f32),
            vmem((ITERS, positions, RS, LANES), f32),
            vmem((ITERS, positions, RS, LANES), f32),
            vmem((ITERS, 4, groups, 8, LANES), f32),
            vmem((4, 24, cs + 2 * LANES), f32),
            vmem((positions, RS, cs), f32),
            dma((chunks, n)),
            dma((chunks, n)),
            dma((n,)),
            dma((n,)),
            dma((n,)),
            dma((n,)),
            dma((3 + chunks,)),
            dma((ITERS, 8)),
            dma((ITERS, 8)),
            dma((strips, PARTS)),
            dma((strips, PARTS)),
            dma((strips, PARTS, blocks)),
            dma((strips, PARTS, blocks)),
            dma((PARTS,)),
        ],
        compiler_params=pltpu.CompilerParams(
            collective_id=0, has_side_effects=True, vmem_limit_bytes=40 * 1024 * 1024
        ),
    )(
        present.T.astype(f32).reshape(count),
        kernel.reshape(25),
        pair,
        die_tiles,
        strength,
    )

    return pl.pallas_call(
        functools.partial(residual_kernel, strips, blocks, cs),
        name="residual",
        out_shape=jax.ShapeDtypeStruct((slots, rows, cols), f32),
        grid_spec=pltpu.PrefetchScalarGridSpec(
            num_scalar_prefetch=3,
            grid=(slots,),
            in_specs=[
                pl.BlockSpec((1, rows, cols), lambda i, *_: (i, 0, 0)),
                pl.BlockSpec((strips, blocks, 1, RS, cs), lambda i, pos, *_: (0, 0, pos[i], 0, 0)),
            ],
            out_specs=pl.BlockSpec((1, rows, cols), lambda i, *_: (i, 0, 0)),
        ),
    )(slot_pos, slot_die, present, die_tiles, refer)


def solution(mesh):
    placed = (
        P(("wafer", "die"), None, None),
        P(("wafer", "die")),
        P(("wafer", "die")),
        P("wafer", None),
        P("die", None, None),
        P(),
    )
    return jax.shard_map(
        functools.partial(shards, mesh.shape["die"]),
        mesh=mesh,
        in_specs=placed,
        out_specs=P(("wafer", "die"), None, None),
        check_vma=False,
    )
```

```python
import functools

import jax
import jax.numpy as jnp
from jax import lax
from jax.experimental import pallas as pl
from jax.experimental.pallas import tpu as pltpu
from jax.sharding import PartitionSpec as P

ITERS = 3
RS = 8
LANES = 128
PARTS = 4
HALVES = 2
PER_STEP = 2


def strip_of(q, strips):
    odd = q % 2
    half = q // 2
    return half * (1 - odd) + (strips - 1 - half) * odd


def chip_of(s, strips):
    high = s // (strips // 2)
    return 2 * s * (1 - high) + (2 * (strips - 1 - s) + 1) * high


def greet(n):
    me = lax.axis_index("die")
    barrier = pltpu.get_barrier_semaphore()
    for k in range(1, n):
        pl.semaphore_signal(barrier, inc=1, device_id={"die": (me + k) % n}, device_id_type=pl.DeviceIdType.MESH)
    pl.semaphore_wait(barrier, n - 1)


def remote(src, dst, send, recv, device):
    return pltpu.make_async_remote_copy(
        src_ref=src, dst_ref=dst, send_sem=send, recv_sem=recv,
        device_id={"die": device}, device_id_type=pl.DeviceIdType.MESH,
    )


def refer_kernel(
    n, strips, blocks, cs, dies, positions,
    live, kern, pair, tiles, power, out,
    stacks, strength, pairs, table, where, mean,
    top, bottom, rows_up, rows_down, side_left, side_right, corners, ext, refer,
    send, recv, psend, precv, qsend, qrecv, local, hsend, hrecv, rsend, rrecv, ssend, srecv, own,
):
    me = lax.axis_index("die")
    slots = tiles.shape[0]
    held = power.shape[0]
    chunks = cs // LANES
    s = strip_of(me // blocks, strips)
    c = me % blocks
    groups = positions // 4

    def device(ds, dc):
        return chip_of((s + ds + strips) % strips, strips) * blocks + (c + dc + blocks) % blocks

    def rows_of(peer):
        return pl.ds(pl.multiple_of(strip_of(peer // blocks, strips) * RS, RS), RS)

    def cols_of(peer, start, size):
        return pl.ds(pl.multiple_of((peer % blocks) * cs + start, LANES), size)

    tile_rows = pl.ds(me * slots, slots)
    power_rows = pl.ds(me * held, held)
    greet(n)
    pair_copies = [pltpu.make_async_copy(pair, pairs.at[tile_rows], local.at[0])]
    for k in range(1, n):
        pair_copies.append(remote(pair, pairs.at[tile_rows], qsend.at[k], qrecv.at[k], (me + k) % n))
    for copy in pair_copies:
        copy.start()
    tile_copies = []
    for u in range(chunks):
        wave = [
            pltpu.make_async_copy(
                tiles.at[:, rows_of(me), cols_of(me, u * LANES, LANES)], stacks[u].at[tile_rows], local.at[2 + u]
            )
        ]
        for k in range(1, n):
            peer = (me + k) % n
            wave.append(
                remote(
                    tiles.at[:, rows_of(peer), cols_of(peer, u * LANES, LANES)], stacks[u].at[tile_rows],
                    send.at[u, k], recv.at[u, k], peer,
                )
            )
        for copy in wave:
            copy.start()
        tile_copies.append(wave)
    power_copies = [
        pltpu.make_async_copy(power.at[:, rows_of(me), cols_of(me, 0, cs)], strength.at[power_rows], local.at[1])
    ]
    for k in range(1, n):
        peer = (me + k) % n
        power_copies.append(
            remote(
                power.at[:, rows_of(peer), cols_of(peer, 0, cs)], strength.at[power_rows],
                psend.at[k], precv.at[k], peer,
            )
        )
    for copy in power_copies:
        copy.start()

    for copy in pair_copies:
        copy.wait()
    order = lax.broadcasted_iota(jnp.int32, (n * slots, LANES), 0)
    target = lax.broadcasted_iota(jnp.int32, (n * slots, LANES), 1)
    for w in range(table.shape[0]):
        hit = pairs[...] == target + w * LANES
        table[w : w + 1, :] = jnp.max(jnp.where(hit, order, 0), axis=0, keepdims=True)
    fetch = pltpu.make_async_copy(table, where, local.at[2 + chunks])
    fetch.start()
    fetch.wait()

    def value_of(p, d, some):
        q = p * dies + d
        entry = where[q // LANES, q % LANES]
        if len(some) == 1:
            return stacks[some[0]][entry]
        return jnp.concatenate([stacks[u][entry] for u in some], axis=1)

    first = pl.ds(0, LANES)
    last = pl.ds(cs - LANES, LANES)
    taps = [[kern[5 * a + b] for b in range(5)] for a in range(5)]
    total = taps[0][0]
    for a in range(5):
        for b in range(5):
            if a or b:
                total = total + taps[a][b]

    def exchange(k, h):
        size = groups // HALVES
        g = pl.ds(h * size, size)
        p = pl.ds(h * size * 4, size * 4)
        moves = [
            (bottom.at[k, g], rows_up.at[k, g], 1, 0),
            (top.at[k, g], rows_down.at[k, g], -1, 0),
            (mean.at[k, p, :, last], side_left.at[k, p], 0, 1),
            (mean.at[k, p, :, first], side_right.at[k, p], 0, -1),
            (bottom.at[k, g, :, last], corners.at[k, 0, g], 1, 1),
            (bottom.at[k, g, :, first], corners.at[k, 1, g], 1, -1),
            (top.at[k, g, :, last], corners.at[k, 2, g], -1, 1),
            (top.at[k, g, :, first], corners.at[k, 3, g], -1, -1),
        ]
        copies = [
            remote(src, dst, hsend.at[k, h, m], hrecv.at[k, h, m], device(ds, dc))
            for m, (src, dst, ds, dc) in enumerate(moves)
        ]
        for copy in copies:
            copy.start()
        return copies

    def guard(flag, x):
        return jnp.where(flag, x, jnp.zeros_like(x))

    has_up, has_down, has_left, has_right = s > 0, s < strips - 1, c > 0, c < blocks - 1
    body = pl.ds(LANES, cs)
    right = pl.ds(LANES + cs, LANES)

    def smooth(k, g, j):
        p = 4 * g + j
        pair = pl.ds(2 * j, 2)
        field = mean[k, p]
        ext[j, 6:8, first] = guard(has_up & has_left, corners[k, 0, g, pair, :])
        ext[j, 6:8, body] = guard(has_up, rows_up[k, g, pair, :])
        ext[j, 6:8, right] = guard(has_up & has_right, corners[k, 1, g, pair, :])
        ext[j, 8:16, first] = guard(has_left, side_left[k, p])
        ext[j, 8:16, body] = field
        ext[j, 8:16, right] = guard(has_right, side_right[k, p])
        ext[j, 16:18, first] = guard(has_down & has_left, corners[k, 2, g, pair, :])
        ext[j, 16:18, body] = guard(has_down, rows_down[k, g, pair, :])
        ext[j, 16:18, right] = guard(has_down & has_right, corners[k, 3, g, pair, :])
        shifted = [ext[j, 6 + a : 14 + a, :] for a in range(5)]
        width = cs + 2 * LANES
        acc = None
        for b in range(5):
            part = shifted[0] * taps[0][b]
            for a in range(1, 5):
                part = part + shifted[a] * taps[a][b]
            if b != 2:
                part = pltpu.roll(part, (2 - b) % width, 1)
            part = part[:, LANES : LANES + cs]
            acc = part if acc is None else acc + part
        power_p = strength[p]
        return (field + power_p * acc) / (1.0 + power_p * total)

    def huber(k, g, j, ref, some):
        lanes = pl.ds(some[0] * LANES, len(some) * LANES)
        p = 4 * g + j
        num = None
        for d in range(dies):
            value = value_of(p, d, some)
            weight = live[p * dies + d] / jnp.maximum(jnp.abs(value - ref), 1.5)
            num, den = (weight * value, weight) if num is None else (num + weight * value, den + weight)
        field = num / den
        mean[k, p, :, lanes] = field
        top[k, g, 2 * j : 2 * j + 2, lanes] = field[0:2]
        bottom[k, g, 2 * j : 2 * j + 2, lanes] = field[RS - 2 : RS]

    for u in range(chunks):
        some = (u,)
        for copy in tile_copies[u]:
            copy.wait()

        @pl.loop(0, groups)
        def _(g):
            for j in range(4):
                p = 4 * g + j
                count = live[p * dies]
                num = count * value_of(p, 0, some)
                for d in range(1, dies):
                    share = live[p * dies + d]
                    count = count + share
                    num = num + share * value_of(p, d, some)
                huber(0, g, j, num / jnp.full(num.shape, count), some)

    halo = [exchange(0, h) for h in range(HALVES)]
    for copy in power_copies:
        copy.wait()
    for k in range(1, ITERS):
        later = []
        for h in range(HALVES):
            for copy in halo[h]:
                copy.wait()

            @pl.loop(h * groups // HALVES, (h + 1) * groups // HALVES)
            def _(g):
                for j in range(4):
                    huber(k, g, j, smooth(k - 1, g, j), tuple(range(chunks)))

            later.append(exchange(k, h))
        halo = later

    turn = 1 - 2 * (c % 2)
    ahead = device(turn, 0)
    parts = rsend.shape[1]
    span = positions // parts
    pending = []
    rings = {}
    mine = []

    def forward(t, h):
        strip = (s - turn * t + strips) % strips
        part = pl.ds(h * span, span)
        target = out.at[strip, c, part]
        block = target if t else refer.at[part]
        if t:
            rings[t - 1, h].wait_recv()
        copies = [remote(block, target, ssend.at[t, h, b], srecv.at[t, h, b], device(0, b)) for b in range(1, blocks)]
        if t < strips - 1:
            rings[t, h] = remote(block, target, rsend.at[t, h], rrecv.at[t, h], ahead)
            copies.insert(0, rings[t, h])
        for copy in copies:
            copy.start()
        pending.extend(copies)

    for h in range(parts):
        if h * HALVES % parts == 0:
            for copy in halo[h * HALVES // parts]:
                copy.wait()

        @pl.loop(h * span // 4, (h + 1) * span // 4)
        def _(g):
            for j in range(4):
                refer[4 * g + j] = smooth(ITERS - 1, g, j)

        part = pl.ds(h * span, span)
        mine.append(pltpu.make_async_copy(refer.at[part], out.at[s, c, part], own.at[h]))
        mine[-1].start()
        forward(0, h)
    for t in range(1, strips):
        for h in range(parts):
            forward(t, h)
    for copy in pending:
        copy.wait_send()
    for t in range(strips):
        for h in range(parts):
            for b in range(1, blocks):
                source = (c - b + blocks) % blocks
                strip = (s - (1 - 2 * (source % 2)) * t + strips) % strips
                target = out.at[strip, source, pl.ds(h * span, span)]
                remote(target, target, ssend.at[t, h, b], srecv.at[t, h, b], device(0, b)).wait_recv()
    for copy in mine:
        copy.wait()


def residual_kernel(strips, blocks, cs, pos, die, present, tile, *rest):
    out = rest[-1]
    for u in range(PER_STEP):
        slot = pl.program_id(0) * PER_STEP + u
        keep = present[die[slot], pos[slot]].astype(jnp.float32)
        for s in range(strips):
            for c in range(blocks):
                rows, cols = pl.ds(s * RS, RS), pl.ds(c * cs, cs)
                out[u, rows, cols] = keep * (tile[u, rows, cols] - rest[u][s, c, 0])


def refer_spec(strips, blocks, cs, u):
    return pl.BlockSpec((strips, blocks, 1, RS, cs), lambda i, pos, *_: (0, 0, pos[i * PER_STEP + u], 0, 0))


def shards(n, die_tiles, slot_pos, slot_die, present, strength, kernel):
    slots, rows, cols = die_tiles.shape
    dies, positions = present.shape
    strips = rows // RS
    blocks = n // strips
    cs = cols // blocks
    hbm = pl.BlockSpec(memory_space=pltpu.HBM)
    smem = pl.BlockSpec(memory_space=pltpu.SMEM)
    dma = pltpu.SemaphoreType.DMA
    f32 = jnp.float32

    count = positions * dies
    chunks = cs // LANES
    pair = jnp.broadcast_to((slot_pos * dies + slot_die)[:, None], (slots, LANES))
    groups = positions // 4
    vmem = pltpu.VMEM
    refer = pl.pallas_call(
        functools.partial(refer_kernel, n, strips, blocks, cs, dies, positions),
        name="refer",
        out_shape=jax.ShapeDtypeStruct((strips, blocks, positions, RS, cs), f32),
        in_specs=[smem, smem, pl.BlockSpec(memory_space=pltpu.VMEM), hbm, hbm],
        out_specs=hbm,
        scratch_shapes=[
            tuple(vmem((n * slots, RS, LANES), f32) for _ in range(chunks)),
            vmem((positions, RS, cs), f32),
            vmem((n * slots, LANES), jnp.int32),
            vmem((count // LANES, LANES), jnp.int32),
            pltpu.SMEM((count // LANES, LANES), jnp.int32),
            vmem((ITERS, positions, RS, cs), f32),
            vmem((ITERS, groups, 8, cs), f32),
            vmem((ITERS, groups, 8, cs), f32),
            vmem((ITERS, groups, 8, cs), f32),
            vmem((ITERS, groups, 8, cs), f32),
            vmem((ITERS, positions, RS, LANES), f32),
            vmem((ITERS, positions, RS, LANES), f32),
            vmem((ITERS, 4, groups, 8, LANES), f32),
            vmem((4, 24, cs + 2 * LANES), f32),
            vmem((positions, RS, cs), f32),
            dma((chunks, n)),
            dma((chunks, n)),
            dma((n,)),
            dma((n,)),
            dma((n,)),
            dma((n,)),
            dma((3 + chunks,)),
            dma((ITERS, HALVES, 8)),
            dma((ITERS, HALVES, 8)),
            dma((strips, PARTS)),
            dma((strips, PARTS)),
            dma((strips, PARTS, blocks)),
            dma((strips, PARTS, blocks)),
            dma((PARTS,)),
        ],
        compiler_params=pltpu.CompilerParams(
            collective_id=0, has_side_effects=True, vmem_limit_bytes=56 * 1024 * 1024
        ),
    )(
        present.T.astype(f32).reshape(count),
        kernel.reshape(25),
        pair,
        die_tiles,
        strength,
    )

    return pl.pallas_call(
        functools.partial(residual_kernel, strips, blocks, cs),
        name="residual",
        out_shape=jax.ShapeDtypeStruct((slots, rows, cols), f32),
        grid_spec=pltpu.PrefetchScalarGridSpec(
            num_scalar_prefetch=3,
            grid=(slots // PER_STEP,),
            in_specs=[
                pl.BlockSpec((PER_STEP, rows, cols), lambda i, *_: (i, 0, 0)),
                *[refer_spec(strips, blocks, cs, u) for u in range(PER_STEP)],
            ],
            out_specs=pl.BlockSpec((PER_STEP, rows, cols), lambda i, *_: (i, 0, 0)),
        ),
        compiler_params=pltpu.CompilerParams(vmem_limit_bytes=56 * 1024 * 1024),
    )(slot_pos, slot_die, present, die_tiles, *[refer] * PER_STEP)


def solution(mesh):
    placed = (
        P(("wafer", "die"), None, None),
        P(("wafer", "die")),
        P(("wafer", "die")),
        P("wafer", None),
        P("die", None, None),
        P(),
    )
    return jax.shard_map(
        functools.partial(shards, mesh.shape["die"]),
        mesh=mesh,
        in_specs=placed,
        out_specs=P(("wafer", "die"), None, None),
        check_vma=False,
    )
```
